128 devices in a mesh: row: 16 (over z, y), col: 8 (over x, core).
Axes of the slice: x: 4, y: 4, z: 4, core: 2. Of those that a mesh axis runs over, the one named last changes fastest.
Arguments:
- acc_feats: float32 [32768, 512], P(('row', 'col')), may hold values from -6 to 6
- content_feats: float32 [16384, 512], P('col', 'row'), may hold values from -6 to 6
- block_values: float32 [16, 8, 128, 128, 128], P('row', 'col'), may hold values from 0.02 to 1
- block_rows: int32 [16, 8, 128], P('row', 'col'), may hold values from 0 to 15, as said below
- block_cols: int32 [16, 8, 128], P('row', 'col'), may hold values from 0 to 15, as said below
- block_count: int32 [16, 8], P('row', 'col'), may hold values from 16 to 128, as said below
- w_self: float32 [512, 512], replicated, may hold values from -0.25 to 0.25
- w_neigh: float32 [512, 512], replicated, may hold values from -0.25 to 0.25
- out_grad: float32 [32768, 512], P(('row', 'col')), may hold values from -6 to 6
Outputs:
- layer_out: float32 [32768, 512], P(('row', 'col'))
- grad_acc: float32 [32768, 512], P(('row', 'col'))
- grad_content: float32 [16384, 512], P('col', 'row')
- grad_self: float32 [512, 512], replicated
- grad_neigh: float32 [512, 512], replicated
The draws below stay inside these ranges and needn't reach their ends.
Inputs may be any that keep to these rules, and one draw needn't show every extreme that they name: `block_count`: exactly one device has 128 live slots; every other device has between 16 and 64. `block_rows`: the slots of one device hold distinct (block row, block column) positions; slots at or beyond the device's count are not part of the adjacency. `block_cols`: see block_rows.
All inputs are finite; a program needn't handle non-finite values.
Results may differ from the reference program's by a relative error of at most 0.0003.
Values sent between devices are 32-bit elements; how exact they have to be, the bound alone decides.
No kernel may reach another device: no remote copies, remote signals or barrier semaphores. Data moves between devices by JAX's collectives and lax.ppermute only.
A program may use at most 128 MiB of HBM per device.

```python
import math
import jax
import jax.numpy as jnp
from jax import lax

F = 512
BLK = 128
BR = 16
BC = 16
CAP = 128
ACC = 32768
CONTENT = 16384
N_ROW = 16
N_COL = 8


def block_layout(key):
    sub_key = jax.random.fold_in(key, 7)
    device_keys = jax.random.split(sub_key, N_ROW * N_COL)

    def one_device(device_key):
        return jax.random.permutation(device_key, BR * BC)[:CAP]
    places = jax.vmap(one_device)(device_keys)
    return places.reshape(N_ROW, N_COL, CAP).astype(jnp.int32)


def draw_block_rows(key, part):
    return block_layout(key) // BC


def draw_block_cols(key, part):
    return block_layout(key) % BC


def draw_block_count(key, part):
    lowest = max(1, CAP // 8)
    upper_bound = max(lowest + 1, CAP // 2 + 1)
    counts = jax.random.randint(jax.random.fold_in(key, 11), (N_ROW * N_COL,), lowest, upper_bound, dtype=jnp.int32)
    busiest = jax.random.randint(jax.random.fold_in(key, 12), (), 0, N_ROW * N_COL, dtype=jnp.int32)
    counts = jnp.where(jnp.arange(N_ROW * N_COL, dtype=jnp.int32) == busiest, CAP, counts)
    return counts.reshape(N_ROW, N_COL).astype(jnp.int32)


def level_of(stream_key, extent, shards, least, high):
    level = 1.0
    for position, blocks in shards:
        heights = jax.random.uniform(jax.random.fold_in(jax.random.fold_in(stream_key, 6), position), (blocks,), jnp.float32, least / len(shards), high / len(shards))
        level = level * jnp.repeat(jnp.exp(heights), extent[position] // blocks).reshape((-1,) + (1,) * (len(extent) - 1 - position))
    return level


def normal_values(rng, extent, deviation, most, cuts=(), kind=jnp.bfloat16):
    entries = jax.random.normal(rng, extent, jnp.float32) * deviation
    if len(cuts) > 0:
        entries = level_of(rng, extent, cuts, -0.22, 0.18) * entries
    return jnp.clip(entries, min=-most, max=most).astype(kind)


def setup_inputs(seed: int = 0) -> dict:
    seeds = jax.random.split(jax.random.key(seed), 10)
    acc_feats = normal_values(seeds[0], (ACC, F), 1.0, 6.0, ((0, 128),), jnp.float32)
    content_feats = normal_values(seeds[1], (CONTENT, F), 1.0, 6.0, ((0, 8), (1, 16)), jnp.float32)
    block_values = jnp.clip(jnp.exp(math.log(1.0) - 3.912023 * jax.random.uniform(seeds[2], (N_ROW, N_COL, CAP, BLK, BLK), jnp.float32) ** level_of(seeds[2], (N_ROW, N_COL, CAP, BLK, BLK), ((0, 16), (1, 8)), -0.2, 0.2)), 0.02, 1.0)
    block_rows = draw_block_rows(jax.random.fold_in(seeds[9], 71), 0)
    block_cols = draw_block_cols(jax.random.fold_in(seeds[9], 71), 0)
    block_count = draw_block_count(jax.random.fold_in(seeds[9], 71), 0)
    w_self = normal_values(seeds[6], (F, F), F ** -0.5, 0.25, (), jnp.float32)
    w_neigh = normal_values(seeds[7], (F, F), F ** -0.5, 0.25, (), jnp.float32)
    out_grad = normal_values(seeds[8], (ACC, F), 1.0, 6.0, ((0, 128),), jnp.float32)
    return {"acc_feats": acc_feats, "content_feats": content_feats, "block_values": block_values, "block_rows": block_rows, "block_cols": block_cols, "block_count": block_count, "w_self": w_self, "w_neigh": w_neigh, "out_grad": out_grad}


highest = lax.Precision.HIGHEST
rms_epsilon = 1e-05

def tile_forward(block_vals, row_ids, col_ids, live_count, source):
    channels = source.shape[1]
    picked = source.reshape(BC, BLK, channels)[col_ids]
    products = jnp.einsum('kij,kjw->kiw', block_vals, picked, precision=highest)
    is_live = jnp.arange(block_vals.shape[0], dtype=jnp.int32) < live_count
    one_hot = ((row_ids[None, :] == jnp.arange(BR, dtype=jnp.int32)[:, None]) & is_live[None, :]).astype(jnp.float32)
    return jnp.einsum('rk,kiw->riw', one_hot, products, precision=highest).reshape(BR * BLK, channels)

def tile_backward(block_vals, row_ids, col_ids, live_count, grad_rows):
    channels = grad_rows.shape[1]
    picked = grad_rows.reshape(BR, BLK, channels)[row_ids]
    products = jnp.einsum('kij,kiw->kjw', block_vals, picked, precision=highest)
    is_live = jnp.arange(block_vals.shape[0], dtype=jnp.int32) < live_count
    one_hot = ((col_ids[None, :] == jnp.arange(BC, dtype=jnp.int32)[:, None]) & is_live[None, :]).astype(jnp.float32)
    return jnp.einsum('ck,kjw->cjw', one_hot, products, precision=highest).reshape(BC * BLK, channels)

def tile_degree(block_vals, row_ids, live_count):
    row_sums = lax.optimization_barrier(jnp.sum(block_vals, axis=2))
    is_live = jnp.arange(block_vals.shape[0], dtype=jnp.int32) < live_count
    one_hot = ((row_ids[None, :] == jnp.arange(BR, dtype=jnp.int32)[:, None]) & is_live[None, :]).astype(jnp.float32)
    return jnp.dot(one_hot, row_sums, precision=highest).reshape(BR * BLK)

def reference(acc_feats, content_feats, block_values, block_rows, block_cols, block_count, w_self, w_neigh, out_grad):
    content_split = content_feats.reshape(N_COL, BC * BLK, F)
    col_range = jnp.arange(N_COL, dtype=jnp.int32)
    row_range = jnp.arange(N_ROW, dtype=jnp.int32)

    def row_shard(row_index):

        def add_column(running, col_index):
            own_values = block_values[row_index, col_index]
            own_rows = block_rows[row_index, col_index]
            own_cols = block_cols[row_index, col_index]
            own_count = block_count[row_index, col_index]
            new_sums = running[0] + tile_forward(own_values, own_rows, own_cols, own_count, content_split[col_index])
            new_degree = running[1] + tile_degree(own_values, own_rows, own_count)
            return ((new_sums, new_degree), None)
        start_value = (jnp.zeros((BR * BLK, F), jnp.float32), jnp.zeros((BR * BLK,), jnp.float32))
        result, _ = lax.scan(add_column, start_value, col_range)
        return result
    summed, degree = lax.map(row_shard, row_range)
    summed = summed.reshape(ACC, F)
    degree = degree.reshape(ACC)
    inv_degree = lax.rsqrt(1.0 + degree)[:, None]
    neigh = summed * inv_degree
    pre_act = jnp.dot(acc_feats, w_self, precision=highest) + jnp.dot(neigh, w_neigh, precision=highest)
    sigmoid_pre = jax.nn.sigmoid(pre_act)
    activation = pre_act * sigmoid_pre
    inv_rms = lax.rsqrt(lax.optimization_barrier(jnp.mean(activation * activation, axis=1, keepdims=True)) + rms_epsilon)
    layer_out = activation * inv_rms
    d_act = (out_grad - layer_out * lax.optimization_barrier(jnp.mean(out_grad * layer_out, axis=1, keepdims=True))) * inv_rms
    d_pre = d_act * sigmoid_pre * (1.0 + pre_act * (1.0 - sigmoid_pre))
    grad_acc = jnp.dot(d_pre, w_self.T, precision=highest)
    d_gathered = jnp.dot(d_pre, w_neigh.T, precision=highest) * inv_degree
    grad_split = d_gathered.reshape(N_ROW, BR * BLK, F)

    def col_shard(col_index):

        def add_row(running, row_index):
            term = tile_backward(block_values[row_index, col_index], block_rows[row_index, col_index], block_cols[row_index, col_index], block_count[row_index, col_index], grad_split[row_index])
            return (running + term, None)
        result, _ = lax.scan(add_row, jnp.zeros((BC * BLK, F), jnp.float32), row_range)
        return result
    grad_content = lax.map(col_shard, col_range).reshape(CONTENT, F)
    norm_factor = 1.0 / math.sqrt(ACC)
    grad_self = jnp.dot(acc_feats.T, d_pre, precision=highest) * norm_factor
    grad_neigh = jnp.dot(neigh.T, d_pre, precision=highest) * norm_factor
    return (layer_out, grad_acc, grad_content, grad_self, grad_neigh)
```

```python
import functools
import math

import jax
import jax.numpy as jnp
from jax import lax
from jax.experimental import pallas as pl
from jax.experimental.pallas import tpu as pltpu
from jax.sharding import PartitionSpec as P

F = 512
BLK = 128
BR = 16
BC = 16
NODES = BR * BLK
CAP = 128
SHARD = 256
GROUP = 64
PIECE = 16
rms_epsilon = 1e-05
f32 = jnp.float32
bf16 = jnp.bfloat16
DELTAS = (0, 1, -1, 2)
VMEM_MB = 1024 * 1024


def y_perm(d):
    return [(z * 4 + y, z * 4 + (y + d) % 4) for z in range(4) for y in range(4)]


def z_perm(d):
    return [(z * 4 + y, ((z + d) % 4) * 4 + y) for z in range(4) for y in range(4)]


def x_perm(d):
    return [(x * 2 + k, ((x + d) % 4) * 2 + k) for x in range(4) for k in range(2)]


CORE_SWAP = [(x * 2 + k, x * 2 + 1 - k) for x in range(4) for k in range(2)]


def send_y(v, d):
    return lax.ppermute(v, "row", y_perm(d))


def send_z(v, d):
    return lax.ppermute(v, "row", z_perm(d))


def send_x(v, d):
    return lax.ppermute(v, "col", x_perm(d))


def swap_core(v):
    return lax.ppermute(v, "col", CORE_SWAP)


def split2(v):
    hi = v.astype(bf16)
    lo = (v - hi.astype(f32)).astype(bf16)
    return hi, lo


def nn(a, b):
    return lax.dot_general(a, b, (((1,), (0,)), ((), ())), preferred_element_type=f32)


def nt(a, b):
    return lax.dot_general(a, b, (((1,), (1,)), ((), ())), preferred_element_type=f32)


def dot3(dot, a, b):
    ah, al = split2(a)
    bh, bl = split2(b)
    return dot(ah, bh) + (dot(al, bh) + dot(ah, bl))


def cost(flops, nbytes):
    return pl.CostEstimate(flops=flops, bytes_accessed=nbytes, transcendentals=0)


def build_kernel(rows, cols, count, vals, hi_ref, lo_ref, table):
    strip = pl.program_id(0)

    @pl.when(strip == 0)
    def _():
        def clear(i, c):
            table[i] = -1
            return c

        lax.fori_loop(0, BR * BC, clear, 0)

        def fill(k, c):
            table[rows[k] * BC + cols[k]] = k
            return c

        lax.fori_loop(0, count[0], fill, 0)

    for c in range(BC):
        slot = table[strip * BC + c]
        a = vals[jnp.maximum(slot, 0)]
        a = jnp.where(slot >= 0, a, 0.0)
        hi, lo = split2(a)
        hi_ref[:, c * BLK : (c + 1) * BLK] = hi
        lo_ref[:, c * BLK : (c + 1) * BLK] = lo


def build_dense(vals, rows, cols, count):
    spec = pl.BlockSpec((BLK, NODES), lambda i, *_: (i, 0))
    shape = jax.ShapeDtypeStruct((NODES, NODES), bf16)
    return pl.pallas_call(
        build_kernel,
        out_shape=(shape, shape),
        grid_spec=pltpu.PrefetchScalarGridSpec(
            num_scalar_prefetch=3,
            grid=(BR,),
            in_specs=[
                pl.BlockSpec(
                    (CAP, BLK, BLK), lambda i, *_: (0, 0, 0), pipeline_mode=pl.Buffered(1)
                )
            ],
            out_specs=(spec, spec),
            scratch_shapes=[pltpu.SMEM((BR * BC,), jnp.int32)],
        ),
        compiler_params=pltpu.CompilerParams(vmem_limit_bytes=16 * VMEM_MB),
        cost_estimate=cost(0, 24 * VMEM_MB),
        name="build_dense",
    )(rows, cols, count, vals)


def forward_kernel(n, ones, idx, *refs):
    pieces = refs[:n]
    dhi, dlo, out, xs = refs[n:]
    m = n * GROUP

    @pl.when(pl.program_id(0) == 0)
    def _():
        for p in range(n):
            hi, lo = split2(pieces[p][...])
            xs[p * GROUP : (p + 1) * GROUP, :] = lo
            xs[m + p * GROUP : m + (p + 1) * GROUP, :] = hi
        if ones:
            xs[2 * m :, :] = jnp.ones((ones, NODES), bf16)

    big = nt(xs[...], dhi[...])
    small = nt(xs[m:, :], dlo[...])
    out[0, :m, :] = big[:m] + big[m : 2 * m] + small[:m]
    if ones:
        out[0, m : m + 8, :] = big[2 * m : 2 * m + 8] + small[m : m + 8]


def forward_product(pieces, dhi, dlo, idx, ones):
    n = len(pieces)
    m = n * GROUP
    tiles = idx.shape[0]
    whole = pl.BlockSpec((GROUP, NODES), lambda i, *_: (0, 0), pipeline_mode=pl.Buffered(1))
    strip = pl.BlockSpec((SHARD, NODES), lambda i, idx: (idx[i], 0))
    rows_out = m + (8 if ones else 0)
    return pl.pallas_call(
        functools.partial(forward_kernel, n, 16 if ones else 0),
        out_shape=jax.ShapeDtypeStruct((tiles, rows_out, SHARD), f32),
        grid_spec=pltpu.PrefetchScalarGridSpec(
            num_scalar_prefetch=1,
            grid=(tiles,),
            in_specs=[whole] * n + [strip, strip],
            out_specs=pl.BlockSpec((1, rows_out, SHARD), lambda i, *_: (i, 0, 0)),
            scratch_shapes=[pltpu.VMEM((2 * m + (16 if ones else 0), NODES), bf16)],
        ),
        compiler_params=pltpu.CompilerParams(vmem_limit_bytes=24 * VMEM_MB),
        cost_estimate=cost(
            6 * m * NODES * SHARD * tiles, tiles * 2 * VMEM_MB + m * NODES * 4
        ),
        name=f"forward_{n}_{int(ones)}",
    )(idx, *pieces, dhi, dlo)


def backward_kernel(n, acc_in, groups, chips, pos, *refs):
    g = refs[: 2 * n]
    refs = refs[2 * n :]
    dhi = refs[:n]
    dlo = refs[n : 2 * n]
    refs = refs[2 * n :]
    if acc_in:
        acc_ref = refs[0]
        refs = refs[1:]
    n_out = 8 if groups else 1
    outs = refs[:n_out]
    ghi, glo = refs[n_out : n_out + 2]

    @pl.when(pl.program_id(0) == 0)
    def _():
        for c in range(n):
            for own in range(2):
                side = pos[0] if own == 0 else 1 - pos[0]
                off = pl.multiple_of(side * SHARD, SHARD)
                hi, lo = split2(g[2 * c + own][...])
                ghi[c, :, pl.ds(off, SHARD)] = hi
                glo[c, :, pl.ds(off, SHARD)] = lo

    total = acc_ref[...] if acc_in else None
    for c in range(n):
        term = nn(ghi[c], dhi[c][...]) + nn(glo[c], dhi[c][...]) + nn(ghi[c], dlo[c][...])
        total = term if total is None else total + term
    if not groups:
        outs[0][...] = total
        return
    full = refs[n_out + 2]
    full[...] = total
    for half in range(2):
        for i, d in enumerate(DELTAS):
            off = half * SHARD + lax.rem(pos[1 + half] + d + 4, 4) * GROUP
            outs[half * 4 + i][...] = full[pl.ds(pl.multiple_of(off, GROUP), GROUP), :]


def backward_product(sources, chips, pos, dhi, dlo, acc, groups):
    n = len(sources) // 2
    tj = 512
    in_specs = [pl.BlockSpec((F, SHARD), lambda i, *_: (0, 0), pipeline_mode=pl.Buffered(1))] * (
        2 * n
    )
    strips = [
        pl.BlockSpec((2 * SHARD, tj), lambda i, chips, pos, c=c: (chips[c], i)) for c in range(n)
    ]
    in_specs = in_specs + strips + strips
    operands = list(sources) + [dhi] * n + [dlo] * n
    tile = pl.BlockSpec((F, tj), lambda i, *_: (0, i))
    if acc is not None:
        in_specs.append(tile)
        operands.append(acc)
    scratch = [pltpu.VMEM((n, F, 2 * SHARD), bf16), pltpu.VMEM((n, F, 2 * SHARD), bf16)]
    if groups:
        out_shape = tuple([jax.ShapeDtypeStruct((GROUP, NODES), f32)] * 8)
        out_specs = tuple([pl.BlockSpec((GROUP, tj), lambda i, *_: (0, i))] * 8)
        scratch.append(pltpu.VMEM((F, tj), f32))
    else:
        out_shape = jax.ShapeDtypeStruct((F, NODES), f32)
        out_specs = tile
    return pl.pallas_call(
        functools.partial(backward_kernel, n, acc is not None, groups),
        out_shape=out_shape,
        grid_spec=pltpu.PrefetchScalarGridSpec(
            num_scalar_prefetch=2,
            grid=(NODES // tj,),
            in_specs=in_specs,
            out_specs=out_specs,
            scratch_shapes=scratch,
        ),
        compiler_params=pltpu.CompilerParams(vmem_limit_bytes=32 * VMEM_MB),
        cost_estimate=cost(
            6 * F * 2 * SHARD * NODES * n, n * 4 * VMEM_MB + (8 if acc is not None else 4) * VMEM_MB
        ),
        name=f"backward_{n}_{int(groups)}",
    )(chips, pos, *operands)


def dense_kernel(pos, *refs):
    c0 = refs[0:4]
    c1 = refs[4:8]
    acc_t, ws_t, wn_t, wn, og_t = refs[8:13]
    lay_t, dpre_t, g_t, neigh_t = refs[13:17]
    m0 = 6 * GROUP
    deg = c0[0][m0 : m0 + 1] + c0[1][m0 : m0 + 1] + c0[2][m0 : m0 + 1] + c0[3][m0 : m0 + 1]
    inv = lax.rsqrt(1.0 + deg)

    def place(refs4, slot, half, origin):
        r = pl.ds(slot * GROUP, GROUP)
        v = refs4[0][r, :] + refs4[1][r, :] + refs4[2][r, :] + refs4[3][r, :]
        off = half * SHARD + lax.rem(pos[1 + half] + origin + 4, 4) * GROUP
        neigh_t[pl.ds(pl.multiple_of(off, GROUP), GROUP), :] = v * inv

    for i, origin in enumerate((0, -1, 1)):
        place(c0, 2 * i, 0, origin)
        place(c0, 2 * i + 1, 1, origin)
    place(c1, 0, 0, 2)
    place(c1, 1, 1, 2)
    pre = dot3(nn, ws_t[...], acc_t[...]) + dot3(nn, wn_t[...], neigh_t[...])
    sig = 1.0 / (1.0 + jnp.exp(-pre))
    act = pre * sig
    rms = lax.rsqrt(jnp.mean(act * act, axis=0, keepdims=True) + rms_epsilon)
    lay = act * rms
    lay_t[...] = lay
    og = og_t[...]
    d_act = (og - lay * jnp.mean(og * lay, axis=0, keepdims=True)) * rms
    dpre = d_act * sig * (1.0 + pre * (1.0 - sig))
    dpre_t[...] = dpre
    g_t[...] = dot3(nn, wn[...], dpre) * inv


def dense_stage(pos, c0, c1, acc_t, ws_t, wn_t, wn, og_t):
    shape = jax.ShapeDtypeStruct((F, SHARD), f32)
    vm = pl.BlockSpec(memory_space=pltpu.VMEM)
    return pl.pallas_call(
        dense_kernel,
        out_shape=(shape,) * 4,
        in_specs=[pl.BlockSpec(memory_space=pltpu.SMEM)] + [vm] * 13,
        out_specs=(vm,) * 4,
        compiler_params=pltpu.CompilerParams(vmem_limit_bytes=32 * VMEM_MB),
        cost_estimate=cost(18 * F * F * SHARD, 12 * VMEM_MB),
        name="dense_stage",
    )(pos, *c0, *c1, acc_t, ws_t, wn_t, wn, og_t)


def fold_kernel(pos, *refs):
    a_in, b_in, a_out, b_out = refs[0:4], refs[4:8], refs[8:12], refs[12:16]
    full = refs[16]
    for ins, outs, p in ((a_in, a_out, pos[2]), (b_in, b_out, pos[1])):
        full[...] = ins[0][...] + ins[1][...] + ins[2][...] + ins[3][...]
        for i, d in enumerate(DELTAS):
            off = lax.rem(p + d + 4, 4) * PIECE
            outs[i][...] = full[pl.ds(pl.multiple_of(off, PIECE), PIECE), :]


def fold_groups(pos, a_in, b_in):
    tj = 1024
    spec_in = pl.BlockSpec((GROUP, tj), lambda i, *_: (0, i))
    spec_out = pl.BlockSpec((PIECE, tj), lambda i, *_: (0, i))
    outs = pl.pallas_call(
        fold_kernel,
        out_shape=(jax.ShapeDtypeStruct((PIECE, NODES), f32),) * 8,
        grid_spec=pltpu.PrefetchScalarGridSpec(
            num_scalar_prefetch=1,
            grid=(NODES // tj,),
            in_specs=[spec_in] * 8,
            out_specs=(spec_out,) * 8,
            scratch_shapes=[pltpu.VMEM((GROUP, tj), f32)],
        ),
        compiler_params=pltpu.CompilerParams(vmem_limit_bytes=16 * VMEM_MB),
        cost_estimate=cost(0, 5 * VMEM_MB),
        name="fold_groups",
    )(pos, *a_in, *b_in)
    return outs[:4], outs[4:]


def join_kernel(pos, *refs):
    a_in, b_in, a_out, b_out = refs[0:4], refs[4:8], refs[8], refs[9]
    for ins, out, p in ((a_in, a_out, pos[2]), (b_in, b_out, pos[1])):
        for i, origin in enumerate((0, -1, 1, 2)):
            off = lax.rem(p + origin + 4, 4) * PIECE
            out[pl.ds(pl.multiple_of(off, PIECE), PIECE), :] = ins[i][...]


def join_pieces(pos, a_in, b_in):
    tj = 1024
    spec_out = pl.BlockSpec((GROUP, tj), lambda i, *_: (0, i))
    spec_in = pl.BlockSpec((PIECE, tj), lambda i, *_: (0, i))
    return pl.pallas_call(
        join_kernel,
        out_shape=(jax.ShapeDtypeStruct((GROUP, NODES), f32),) * 2,
        grid_spec=pltpu.PrefetchScalarGridSpec(
            num_scalar_prefetch=1,
            grid=(NODES // tj,),
            in_specs=[spec_in] * 8,
            out_specs=(spec_out,) * 2,
        ),
        compiler_params=pltpu.CompilerParams(vmem_limit_bytes=16 * VMEM_MB),
        cost_estimate=cost(0, 2 * VMEM_MB),
        name="join_pieces",
    )(pos, *a_in, *b_in)


def to_grouped(w):
    v = w.reshape(4, 4, 2, PIECE, F)
    a = v[:, :, 0].reshape(SHARD, F)
    b = v[:, :, 1].transpose(1, 0, 2, 3).reshape(SHARD, F)
    return jnp.concatenate([a, b], axis=0)


def from_grouped(w):
    a = w[:SHARD].reshape(4, 4, 1, PIECE, F)
    b = w[SHARD:].reshape(4, 4, 1, PIECE, F).transpose(1, 0, 2, 3, 4)
    return jnp.concatenate([a, b], axis=2).reshape(F, F)


def reduce_over_col(partner_part, own_part):
    got = swap_core(partner_part)
    q = [own_part[i] + got[i] for i in range(4)]
    return [q[0]] + [send_x(q[i], d) for i, d in enumerate(DELTAS) if d]


def reduce_weights(wg, x, k, scale):
    w4 = wg.reshape(4, 2, 128, F)
    got = swap_core(lax.dynamic_index_in_dim(w4, 1 - k, 1, keepdims=False))
    q = lax.dynamic_index_in_dim(w4, k, 1, keepdims=False) + got
    parts = [lax.dynamic_index_in_dim(q, (x + d) % 4, 0, keepdims=False) for d in DELTAS]
    got = [parts[0]] + [send_x(parts[i], d) for i, d in enumerate(DELTAS) if d]
    s = got[0] + got[1] + got[2] + got[3]
    t = lax.all_to_all(s, "row", 0, 0, tiled=True)
    mine = jnp.sum(t.reshape(16, 8, F), axis=0) * scale
    r = lax.all_to_all(jnp.tile(mine, (16, 1)), "row", 0, 0, tiled=True)
    ring = [r] + [send_x(r, d) for d in DELTAS if d]
    full = jnp.zeros((4, 128, F), f32)
    for v, origin in zip(ring, (0, -1, 1, 2)):
        full = lax.dynamic_update_slice_in_dim(full, v[None], (x + origin) % 4, 0)
    other = swap_core(full)
    first = jnp.where(k == 0, full, other)
    second = jnp.where(k == 0, other, full)
    whole = jnp.stack([first, second], axis=1).reshape(2 * F, F)
    return whole[:F], from_grouped(whole[F:])


def local(
    acc_feats,
    content_feats,
    block_values,
    block_rows,
    block_cols,
    block_count,
    w_self,
    w_neigh,
    out_grad,
):
    high = lax.Precision.HIGH
    row = lax.axis_index("row")
    col = lax.axis_index("col")
    z, y, x, k = row // 4, row % 4, col // 2, col % 2
    pos = jnp.stack([k, z, y]).astype(jnp.int32)
    order = jnp.array(DELTAS, jnp.int32)
    dest = ((x + order + 4) % 4) * 2
    idx_own = (dest + k).astype(jnp.int32)
    idx_partner = (dest + 1 - k).astype(jnp.int32)

    xt = content_feats.T
    a, b = xt[:PIECE], xt[PIECE:]
    a_in = [a] + [send_y(a, d) for d in DELTAS[1:]]
    b_in = [b] + [send_z(b, d) for d in DELTAS[1:]]
    ag, bg = join_pieces(pos, a_in, b_in)
    near = [ag, bg]
    for d in (1, -1):
        near += [send_z(ag, d), send_y(bg, d)]
    far = [send_z(ag, 2), send_y(bg, 2)]

    dhi, dlo = build_dense(
        block_values[0, 0], block_rows[0, 0], block_cols[0, 0], block_count[0]
    )
    p0 = forward_product(near, dhi, dlo, idx_partner, True)
    o0 = forward_product(near, dhi, dlo, idx_own, True)
    c0 = reduce_over_col(p0, o0)
    p1 = forward_product(far, dhi, dlo, idx_partner, False)
    o1 = forward_product(far, dhi, dlo, idx_own, False)
    c1 = reduce_over_col(p1, o1)

    wn = to_grouped(w_neigh)
    acc_t = acc_feats.T
    lay_t, dpre_t, g_t, neigh_t = dense_stage(
        pos, c0, c1, acc_t, w_self.T, wn.T, wn, out_grad.T
    )

    g_p = swap_core(g_t)
    g_1 = send_x(g_t, 1)
    g_m = send_x(g_t, -1)
    g_2 = send_x(g_t, 2)
    g_1p, g_mp, g_2p = swap_core(g_1), swap_core(g_m), swap_core(g_2)

    def chip(*ds):
        return jnp.stack([(x + d + 4) % 4 for d in ds]).astype(jnp.int32)

    acc1 = backward_product([g_t, g_p], chip(0), pos, dhi, dlo, None, False)
    acc2 = backward_product([g_1, g_1p, g_m, g_mp], chip(-1, 1), pos, dhi, dlo, acc1, False)
    parts = backward_product([g_2, g_2p], chip(2), pos, dhi, dlo, acc2, True)
    a_in = [parts[0]] + [send_z(parts[i], d) for i, d in enumerate(DELTAS) if d]
    b_in = [parts[4]] + [send_y(parts[4 + i], d) for i, d in enumerate(DELTAS) if d]
    a_out, b_out = fold_groups(pos, a_in, b_in)
    a_in = [a_out[0]] + [send_y(a_out[i], d) for i, d in enumerate(DELTAS) if d]
    b_in = [b_out[0]] + [send_z(b_out[i], d) for i, d in enumerate(DELTAS) if d]
    gc_t = jnp.concatenate(
        [a_in[0] + a_in[1] + a_in[2] + a_in[3], b_in[0] + b_in[1] + b_in[2] + b_in[3]], axis=0
    )

    layer_out = lay_t.T
    grad_acc = lax.dot_general(dpre_t, w_self, (((0,), (1,)), ((), ())), precision=high)
    wg = lax.dot_general(
        jnp.concatenate([acc_t, neigh_t], axis=0),
        dpre_t,
        (((1,), (1,)), ((), ())),
        precision=high,
    )
    acc_total = acc_feats.shape[0] * lax.axis_size("row") * lax.axis_size("col")
    grad_self, grad_neigh = reduce_weights(wg, x, k, 1.0 / math.sqrt(acc_total))
    return (layer_out, grad_acc, gc_t.T, grad_self, grad_neigh)


def solution(mesh):
    in_specs = (
        P(("row", "col"), None),
        P("col", "row"),
        P("row", "col", None, None, None),
        P("row", "col", None),
        P("row", "col", None),
        P("row", "col"),
        P(),
        P(),
        P(("row", "col"), None),
    )
    out_specs = (P(("row", "col"), None), P(("row", "col"), None), P("col", "row"), P(), P())
    return jax.shard_map(local, mesh=mesh, in_specs=in_specs, out_specs=out_specs, check_vma=False)
```
